128 devices in a mesh: wide: 16 (over z_lo, x, core), node: 8 (over y, z_hi).
Axes of the slice: x: 4, y: 4, z: 4 (z_hi: 2, z_lo: 2; z = z_hi * 2 + z_lo), core: 2. Of those that a mesh axis runs over, the one named last changes fastest.
Arguments:
- normed: bfloat16 [65536, 4096], P(('wide', 'node')), may hold values from -24 to 24
- queries: bfloat16 [65536, 2048], P(('wide', 'node')), may hold values from -48 to 48
- keys: bfloat16 [65536, 512], P(('wide', 'node')), may hold values from -6 to 6
- values: bfloat16 [65536, 512], P(('wide', 'node')), may hold values from -6 to 6
- attn_grad: bfloat16 [65536, 2048], P(('wide', 'node')), may hold values from -6 to 6
- kv_proj: bfloat16 [4096, 1024], P(None, 'node'), may hold values from -0.09375 to 0.09375
Outputs:
- query_grad: bfloat16 [65536, 2048], P(('wide', 'node'))
- input_grad: bfloat16 [65536, 4096], P(('wide', 'node'))
- weight_grad: float32 [4096, 1024], P(('wide', 'node'))
The draws below stay inside these ranges and needn't reach their ends.
All inputs are finite; a program needn't handle non-finite values.
Results may differ from the reference program's by a relative error of at most 0.019.
Values may be sent and summed in bfloat16 or wider, within the bound.
No kernel may reach another device: no remote copies, remote signals or barrier semaphores. Data moves between devices by JAX's collectives and lax.ppermute only.
A program may use at most 192 MiB of HBM per device.

```python
import jax
import jax.numpy as jnp
from jax import lax

D = 4096
HQ = 16
KVH = 4
HD = 128
TOK_DEV = 512
TOKENS = 65536


def draw_pair(key):
    key_base = jax.random.fold_in(key, 71)
    key_draw, query_draw = jax.random.split(key_base)
    key_vals = jnp.clip(jax.random.normal(key_draw, (TOKENS, KVH, HD), jnp.float32), -6.0, 6.0)
    query_vals = jnp.clip(jax.random.normal(query_draw, (TOKENS, KVH, HQ // KVH, HD), jnp.float32), -6.0, 6.0)
    return (query_vals.reshape(TOKENS, HQ * HD), key_vals.reshape(TOKENS, KVH * HD))


def draw_queries(key, part):
    return draw_pair(key)[0].astype(jnp.bfloat16)


def draw_keys(key, part):
    return draw_pair(key)[1].astype(jnp.bfloat16)


def with_spikes(drawn, key, source, target, shards_of, factor):
    owner, partner = [(jnp.arange(drawn.shape[dim]) // (drawn.shape[dim] // shards_of)).reshape([-1 if axis == dim else 1 for axis in range(drawn.ndim)]) for dim in (source, target)]
    chosen = jax.random.permutation(key, shards_of)[partner]
    strong = (owner == chosen) | (owner == (partner + shards_of // 2) % shards_of)
    return jnp.where(strong, factor * drawn, drawn)


def shard_levels(own_key, dims, cuts, low, top_value):
    loudness = 1.0
    for dim, parts in cuts:
        draws = jax.random.uniform(jax.random.fold_in(jax.random.fold_in(own_key, 6), dim), (parts,), jnp.float32, low / len(cuts), top_value / len(cuts))
        loudness = loudness * jnp.repeat(jnp.exp(draws), dims[dim] // parts).reshape((-1,) + (1,) * (len(dims) - 1 - dim))
    return loudness


def scatter_about(key, dims, scale, bound, cuts=(), kind=jnp.bfloat16):
    level = shard_levels(key, dims, cuts, -0.22, 0.18) if cuts else 1.0
    entries = jax.random.normal(key, dims, jnp.float32) * scale * level
    return jnp.minimum(jnp.maximum(entries, -bound), bound).astype(kind)


def heavy_noise(rng, shape, scale, bound, shards, heavy, kind=jnp.bfloat16):
    drawn = scale * jax.random.normal(rng, shape, jnp.float32)
    if shards:
        drawn = drawn * shard_levels(rng, shape, shards, -0.22, 0.18)
    return jnp.clip(with_spikes(drawn, jax.random.fold_in(rng, 3), *heavy), -bound, bound).astype(kind)


def setup_inputs(seed: int = 0) -> dict:
    arg_keys = jax.random.split(jax.random.key(seed), 7)
    normed = heavy_noise(arg_keys[0], (TOKENS, D), 1.0, 24.0, ((0, 128),), (0, 1, 128, 5.5))
    queries = draw_queries(jax.random.fold_in(arg_keys[6], 71), 0)
    keys = draw_keys(jax.random.fold_in(arg_keys[6], 71), 0)
    values = scatter_about(arg_keys[3], (TOKENS, KVH * HD), 1.0, 6.0, ((0, 128),))
    attn_grad = scatter_about(arg_keys[4], (TOKENS, HQ * HD), 1.0, 6.0, ((0, 128),))
    kv_proj = scatter_about(arg_keys[5], (D, 2 * KVH * HD), D ** -0.5, 0.09375, ((1, 8),))
    return {"normed": normed, "queries": queries, "keys": keys, "values": values, "attn_grad": attn_grad, "kv_proj": kv_proj}


ROPE_BASE = 500000.0


def rope_tables(length, size):
    half_size = size // 2
    frequency = jnp.power(jnp.float32(ROPE_BASE), -jnp.arange(half_size, dtype=jnp.float32) * (2.0 / size))
    angles = jnp.arange(length, dtype=jnp.float32)[:, None] * frequency[None, :]
    cosine = jnp.concatenate([jnp.cos(angles), jnp.cos(angles)], axis=1)
    sine_tab = jnp.concatenate([jnp.sin(angles), jnp.sin(angles)], axis=1)
    return cosine, sine_tab


def sequence_grads(queries, keys, values, attn_grad, cosine, sine_tab):
    length = queries.shape[0]
    query_heads = queries.reshape(length, KVH, HQ // KVH, HD).astype(jnp.float32)
    key_heads = keys.reshape(length, KVH, HD).astype(jnp.float32)
    value_heads = values.reshape(length, KVH, HD).astype(jnp.float32)
    grad_heads = attn_grad.reshape(length, KVH, HQ // KVH, HD).astype(jnp.float32)
    inv_root = HD ** -0.5
    scores = jnp.einsum("tkgd,skd->kgts", query_heads, key_heads) * inv_root
    positions = jnp.arange(length, dtype=jnp.int32)
    causal_mask = positions[:, None] >= positions[None, :]
    scores = jnp.where(causal_mask, scores, -jnp.inf)
    row_max = jnp.max(scores, axis=-1, keepdims=True)
    exponent = jnp.exp(scores - row_max)
    prob_full = exponent / jnp.sum(exponent, axis=-1, keepdims=True)
    prob_low = prob_full.astype(jnp.bfloat16)
    grad_prob = jnp.einsum("tkgd,skd->kgts", grad_heads, value_heads)
    row_delta = jnp.sum(prob_full * grad_prob, axis=-1, keepdims=True)
    grad_score = (prob_full * (grad_prob - row_delta) * inv_root).astype(jnp.bfloat16)
    grad_wide = grad_score.astype(jnp.float32)
    query_grad = jnp.einsum("kgts,skd->tkgd", grad_wide, key_heads).astype(jnp.bfloat16).reshape(length, HQ * HD)
    key_grad = jnp.einsum("kgts,tkgd->skd", grad_wide, query_heads)
    value_grad = jnp.einsum("kgts,tkgd->skd", prob_low.astype(jnp.float32), grad_heads).astype(jnp.bfloat16)
    half_size = HD // 2
    sine_part = key_grad * sine_tab[:, None, :]
    key_unrot = key_grad * cosine[:, None, :] + jnp.concatenate([sine_part[..., half_size:], -sine_part[..., :half_size]], axis=-1)
    kv_grad = jnp.concatenate([key_unrot.astype(jnp.bfloat16).reshape(length, KVH * HD), value_grad.reshape(length, KVH * HD)], axis=1)
    return query_grad, kv_grad


def reference(normed, queries, keys, values, attn_grad, kv_proj):
    seq_count = TOKENS // TOK_DEV
    cosine, sine_tab = rope_tables(TOK_DEV, HD)
    grad_scale = TOKENS ** -0.5

    def per_sequence(accum_grad, seq_index):
        offset = (seq_index * TOK_DEV).astype(jnp.int32)
        normed_seq = lax.dynamic_slice_in_dim(normed, offset, TOK_DEV, 0)
        query_seq = lax.dynamic_slice_in_dim(queries, offset, TOK_DEV, 0)
        key_seq = lax.dynamic_slice_in_dim(keys, offset, TOK_DEV, 0)
        value_seq = lax.dynamic_slice_in_dim(values, offset, TOK_DEV, 0)
        grad_seq = lax.dynamic_slice_in_dim(attn_grad, offset, TOK_DEV, 0)
        query_out, kv_grad = sequence_grads(query_seq, key_seq, value_seq, grad_seq, cosine, sine_tab)
        input_out = jnp.dot(kv_grad, kv_proj.T, preferred_element_type=jnp.float32).astype(jnp.bfloat16)
        accum_grad = accum_grad + jnp.dot(normed_seq.T, kv_grad, preferred_element_type=jnp.float32) * grad_scale
        return accum_grad, (query_out, input_out)

    start_grad = jnp.zeros((D, 2 * KVH * HD), jnp.float32)
    weight_grad, (query_out, input_out) = lax.scan(per_sequence, start_grad, jnp.arange(seq_count, dtype=jnp.int32))
    return query_out.reshape(TOKENS, HQ * HD), input_out.reshape(TOKENS, D), weight_grad
```

```python
import functools

import jax
import jax.numpy as jnp
from jax import lax
from jax.experimental import pallas as pl
from jax.experimental.pallas import tpu as pltpu
from jax.sharding import PartitionSpec as P


KVH = 4
HD = 128
GROUP = 4
ROPE_BASE = 500000.0
LOG2E = 1.4426950408889634
AXES = ("wide", "node")
F32 = jnp.float32
BF = jnp.bfloat16


def permutation(move):
    pairs = []
    for zl in range(2):
        for x in range(4):
            for c in range(2):
                for y in range(4):
                    for zh in range(2):
                        source = ((zl * 4 + x) * 2 + c) * 8 + y * 2 + zh
                        tx, tc, ty, tz = move(x, c, y, zh * 2 + zl)
                        pairs.append((source, (((tz % 2) * 4 + tx) * 2 + tc) * 8 + ty * 2 + tz // 2))
    return pairs


PARTNER = permutation(lambda x, c, y, z: (x, 1 - c, y, z))
Z_HALF = permutation(lambda x, c, y, z: (x, c, y, z ^ 2))
ALONG_Y = {k: permutation(lambda x, c, y, z: (x, c, y ^ k, z)) for k in (1, 2, 3)}
FIRST = {
    k: permutation(lambda x, c, y, z: (x ^ k, c, y, z) if c == 0 else (x, c, y, z ^ k))
    for k in (1, 2, 3)
}
SECOND = {
    k: permutation(lambda x, c, y, z: (x, c, y, z ^ k) if c == 0 else (x ^ k, c, y, z))
    for k in (1, 2, 3)
}


def send(value, pairs):
    return lax.ppermute(value, AXES, pairs)


def rope_tables(length, size):
    half_size = size // 2
    frequency = jnp.power(
        jnp.float32(ROPE_BASE), -jnp.arange(half_size, dtype=jnp.float32) * (2.0 / size)
    )
    angles = jnp.arange(length, dtype=jnp.float32)[:, None] * frequency[None, :]
    cosine = jnp.concatenate([jnp.cos(angles), jnp.cos(angles)], axis=1)
    sine_tab = jnp.concatenate([jnp.sin(angles), jnp.sin(angles)], axis=1)
    return (cosine, sine_tab)


def dot(a, b, da, db):
    return lax.dot_general(a, b, (((da,), (db,)), ((), ())), preferred_element_type=F32)


def attention_kernel(
    place, q_ref, k_ref, v_ref, do_ref, cos_ref, sin_ref, dq_ref, kv_ref, away_ref, dk_acc, dv_acc, *, block
):
    length = q_ref.shape[0]
    inv_root = HD ** (-0.5)
    blocks = length // block
    k = k_ref[...]
    v = v_ref[...]
    rows = lax.broadcasted_iota(jnp.int32, (block, GROUP * block), 0)
    cols = lax.broadcasted_iota(jnp.int32, (block, GROUP * block), 1)
    keep = rows <= lax.rem(cols, block)
    for b in reversed(range(blocks)):
        end = (b + 1) * block
        part = slice(b * block, end)
        queries = jnp.concatenate([q_ref[part, j * HD : (j + 1) * HD] for j in range(GROUP)], axis=0)
        grads = jnp.concatenate([do_ref[part, j * HD : (j + 1) * HD] for j in range(GROUP)], axis=0)
        scores = dot(k[:end], queries, 1, 1)
        grad_prob = dot(v[:end], grads, 1, 1)
        diagonal = jnp.where(keep, scores[end - block :], -jnp.inf)
        if b:
            scores = jnp.concatenate([scores[: end - block], diagonal], axis=0)
        else:
            scores = diagonal
        top = jnp.max(scores, axis=0, keepdims=True)
        exponent = jnp.exp2((scores - top) * (LOG2E * inv_root))
        inv_sum = 1.0 / jnp.sum(exponent, axis=0, keepdims=True)
        delta = jnp.sum(exponent * grad_prob, axis=0, keepdims=True) * inv_sum
        prob_low = (exponent * inv_sum).astype(BF)
        grad_score = (exponent * (grad_prob - delta) * (inv_sum * inv_root)).astype(BF)
        dk = dot(grad_score, queries, 1, 0)
        dv = dot(prob_low, grads, 1, 0)
        if b == blocks - 1:
            dk_acc[...] = dk
            dv_acc[...] = dv
        else:
            dk_acc[:end, :] += dk
            dv_acc[:end, :] += dv
        dq = dot(grad_score, k[:end], 0, 0)
        for j in range(GROUP):
            dq_ref[part, j * HD : (j + 1) * HD] = dq[j * block : (j + 1) * block].astype(BF)
    key_grad = dk_acc[...]
    sine_part = key_grad * sin_ref[...]
    half = HD // 2
    turned = jnp.concatenate([sine_part[:, half:], -sine_part[:, :half]], axis=1)
    key_part = (key_grad * cos_ref[...] + turned).astype(BF)
    value_part = dv_acc[...].astype(BF)
    first = place[0] == 0
    stay = jnp.where(first, key_part, value_part)
    away = jnp.where(first, value_part, key_part)
    kv_ref[0] = stay
    kv_ref[1] = away
    away_ref[...] = away


def attention(place, q, k, v, do, cosine, sine_tab):
    length = q.shape[0]
    width = GROUP * HD
    return pl.pallas_call(
        functools.partial(attention_kernel, block=128),
        grid_spec=pltpu.PrefetchScalarGridSpec(
            num_scalar_prefetch=1,
            grid=(KVH,),
            in_specs=[
                pl.BlockSpec((length, width), lambda g, p: (0, g)),
                pl.BlockSpec((length, HD), lambda g, p: (0, g)),
                pl.BlockSpec((length, HD), lambda g, p: (0, g)),
                pl.BlockSpec((length, width), lambda g, p: (0, g)),
                pl.BlockSpec((length, HD), lambda g, p: (0, 0)),
                pl.BlockSpec((length, HD), lambda g, p: (0, 0)),
            ],
            out_specs=[
                pl.BlockSpec((length, width), lambda g, p: (0, g)),
                pl.BlockSpec((2, length, HD), lambda g, p: (0, 0, g)),
                pl.BlockSpec((length, HD), lambda g, p: (0, g)),
            ],
            scratch_shapes=[pltpu.VMEM((length, HD), F32), pltpu.VMEM((length, HD), F32)],
        ),
        out_shape=[
            jax.ShapeDtypeStruct((length, KVH * width), BF),
            jax.ShapeDtypeStruct((2, length, KVH * HD), BF),
            jax.ShapeDtypeStruct((length, KVH * HD), BF),
        ],
        name="attention",
    )(place, q, k, v, do, cosine, sine_tab)


def weight_kernel(place, na_ref, nb_ref, ka_ref, kb_ref, *outs, scale):
    step = pl.program_id(0)
    c, x, y, z = place[0], place[1], place[2], place[3]
    to_zl = step // 8
    to_x = lax.rem(step // 2, 4)
    to_c = lax.rem(step, 2)
    value = dot(na_ref[...], ka_ref[0], 0, 0) + dot(nb_ref[...], kb_ref[...], 0, 0)
    value = (value * scale).astype(BF).reshape(4, 2, 32, value.shape[1])
    kx = lax.bitwise_xor(to_x, x)
    kc = lax.bitwise_xor(to_c, c)
    for to_zh in range(2):
        kz = lax.bitwise_xor(to_zh * 2 + to_zl, z)
        first = jnp.where(c == 0, kx, kz)
        second = jnp.where(c == 0, kz, kx)
        for k in range(4):

            @pl.when(first == k)
            def _():
                for to_y in range(4):
                    outs[k][second, kc, lax.bitwise_xor(to_y, y)] = value[to_y, to_zh]


def weight_terms(place, own, other, kv, kv_other, scale):
    tokens, width = own.shape
    cols = kv.shape[2]
    rows = width // 16
    shape = (4, 2, 4, 32, cols)
    return pl.pallas_call(
        functools.partial(weight_kernel, scale=scale),
        grid_spec=pltpu.PrefetchScalarGridSpec(
            num_scalar_prefetch=1,
            grid=(16,),
            in_specs=[
                pl.BlockSpec((tokens, rows), lambda i, p: (0, i)),
                pl.BlockSpec((tokens, rows), lambda i, p: (0, i)),
                pl.BlockSpec((1, tokens, cols), lambda i, p: (0, 0, 0)),
                pl.BlockSpec((tokens, cols), lambda i, p: (0, 0)),
            ],
            out_specs=[pl.BlockSpec(shape, lambda i, p: (0, 0, 0, 0, 0)) for _ in range(4)],
        ),
        out_shape=[jax.ShapeDtypeStruct(shape, BF) for _ in range(4)],
        name="weight_terms",
    )(place, own, other, kv, kv_other)


def sum_kernel(*refs):
    ins, outs = refs[:4], refs[4:]
    for k in range(4):
        total = sum(r[:, k].astype(F32) for r in ins)
        outs[k][...] = total.astype(outs[k].dtype)


def summed(arrays, blocks):
    lead, _, m, n = arrays[0].shape
    return pl.pallas_call(
        sum_kernel,
        grid=(blocks,),
        in_specs=[pl.BlockSpec((lead, 4, m // blocks, n), lambda i: (0, 0, i, 0)) for _ in range(4)],
        out_specs=[pl.BlockSpec((lead, m // blocks, n), lambda i: (0, i, 0)) for _ in range(4)],
        out_shape=[jax.ShapeDtypeStruct((lead, m, n), BF) for k in range(4)],
        name="summed",
    )(*arrays)


def input_kernel(place, *refs):
    step = pl.program_id(0)
    kvs, mine, theirs, out_ref = refs[:8], refs[8:16], refs[16:24], refs[24]
    kv = jnp.concatenate([r[0] for r in kvs], axis=1)

    def write(blocks):
        weights = jnp.concatenate([r[...] for r in blocks], axis=1)
        out_ref[...] = dot(kv, weights, 1, 1).astype(BF)

    half = pl.num_programs(0) // 2

    @pl.when(step < half)
    def _():
        write(mine)

    @pl.when(step >= half)
    def _():
        write(theirs)


def input_grads(place, kv, own_proj, mine, theirs):
    length = kv.shape[1]
    depth = own_proj.shape[0]
    tile = 512
    half = depth // tile // 2

    def kv_map(j):
        k, h = j % 4, j // 4

        def index(i, p):
            node = lax.bitwise_xor(p[2], k) * 2 + lax.bitwise_xor(p[4], h)
            return (lax.bitwise_xor(node // 4, p[0]), 0, lax.rem(node, 4))

        return index

    def own_map(i, p):
        return (p[0] * half + jnp.minimum(i, half - 1), 0)

    def other_map(i, p):
        return ((1 - p[0]) * half + jnp.maximum(i - half, 0), 0)

    def out_map(i, p):
        return (0, lax.rem(p[0] * half + i, 2 * half))

    in_specs = [pl.BlockSpec((1, length, HD), kv_map(j)) for j in range(8)]
    in_specs += [pl.BlockSpec((tile, HD), own_map)]
    in_specs += [pl.BlockSpec((tile, HD), lambda i, p: (jnp.minimum(i, half - 1), 0)) for _ in range(7)]
    in_specs += [pl.BlockSpec((tile, HD), other_map)]
    in_specs += [pl.BlockSpec((tile, HD), lambda i, p: (jnp.maximum(i - half, 0), 0)) for _ in range(7)]
    return pl.pallas_call(
        input_kernel,
        grid_spec=pltpu.PrefetchScalarGridSpec(
            num_scalar_prefetch=1,
            grid=(2 * half,),
            in_specs=in_specs,
            out_specs=pl.BlockSpec((length, tile), out_map),
        ),
        out_shape=jax.ShapeDtypeStruct((length, depth), BF),
        name="input_grads",
    )(place, *([kv] * 8), own_proj, *mine, own_proj, *theirs)


def local(normed, queries, keys, values, attn_grad, kv_proj):
    length, width = normed.shape
    wide = lax.axis_index("wide")
    node = lax.axis_index("node")
    c, x, zl = wide % 2, (wide // 2) % 4, wide // 8
    y, zh = node // 2, node % 2
    place = jnp.stack([c, x, y, zh * 2 + zl, zh]).astype(jnp.int32)
    tokens = length * lax.axis_size("wide") * lax.axis_size("node")

    half = lax.dynamic_slice_in_dim(kv_proj, c * (width // 2), width // 2, 0)
    normed_other = send(normed, PARTNER)
    across = send(half, Z_HALF)
    near = [send(half, ALONG_Y[k]) for k in (1, 2, 3)]

    cosine, sine_tab = rope_tables(length, HD)
    query_grad, kv, away = attention(place, queries, keys, values, attn_grad, cosine, sine_tab)
    kv_other = send(away, PARTNER)
    terms = weight_terms(place, normed, normed_other, kv, kv_other, tokens ** (-0.5))
    cols = terms[0].shape[-1]
    got = [terms[0]] + [send(terms[k], FIRST[k]) for k in (1, 2, 3)]

    across_late, _ = lax.optimization_barrier((across, terms[0]))
    far = [send(across_late, ALONG_Y[k]) for k in (1, 2, 3)]
    mine = near + [across] + far
    theirs = [send(block, PARTNER) for block in mine]

    got = summed([g.reshape(1, 4, 256, cols) for g in got], 4)
    got = [got[0]] + [send(got[k], SECOND[k]) for k in (1, 2, 3)]
    got = summed([g.reshape(2, 4, 32, cols) for g in got], 1)
    got = [got[0]] + [send(got[k], ALONG_Y[k]) for k in (1, 2, 3)]
    total = sum(g.astype(F32) for g in got)
    part, other = total[0], send(total[1], PARTNER)
    weight_grad = jnp.where(
        c == 0, jnp.concatenate([part, other], axis=1), jnp.concatenate([other, part], axis=1)
    )
    input_grad = input_grads(place, kv, kv_proj, mine, theirs)
    return (query_grad, input_grad, weight_grad)


def solution(mesh):
    spec = P(("wide", "node"), None)
    return jax.shard_map(
        local,
        mesh=mesh,
        in_specs=(spec, spec, spec, spec, spec, P(None, "node")),
        out_specs=(spec, spec, spec),
        check_vma=False,
    )
```

```python
import functools

import jax
import jax.numpy as jnp
import numpy as np
from jax import lax
from jax.experimental import pallas as pl
from jax.experimental.pallas import tpu as pltpu
from jax.sharding import Mesh
from jax.sharding import PartitionSpec as P


KVH = 4
HD = 128
GROUP = 4
ROPE_BASE = 500000.0
LOG2E = 1.4426950408889634
INPUT_TILE = 1024
ATTENTION_VMEM = 60 << 20
WEIGHT_VMEM = 60 << 20
INPUT_VMEM = 24 << 20
AXES = ("zl", "x", "c", "y", "zh")
F32 = jnp.float32
BF = jnp.bfloat16


def permutation(move):
    pairs = []
    for zl in range(2):
        for x in range(4):
            for c in range(2):
                for y in range(4):
                    for zh in range(2):
                        source = ((zl * 4 + x) * 2 + c) * 8 + y * 2 + zh
                        tx, tc, ty, tz = move(x, c, y, zh * 2 + zl)
                        pairs.append((source, (((tz % 2) * 4 + tx) * 2 + tc) * 8 + ty * 2 + tz // 2))
    return pairs


PARTNER = permutation(lambda x, c, y, z: (x, 1 - c, y, z))
Z_HALF = permutation(lambda x, c, y, z: (x, c, y, z ^ 2))
ALONG_Y = {k: permutation(lambda x, c, y, z: (x, c, y ^ k, z)) for k in (1, 2, 3)}
FIRST = {
    k: permutation(lambda x, c, y, z: (x ^ k, c, y, z) if c == 0 else (x, c, y, z ^ k))
    for k in (1, 2, 3)
}
SECOND = {
    k: permutation(lambda x, c, y, z: (x, c, y, z ^ k) if c == 0 else (x ^ k, c, y, z))
    for k in (1, 2, 3)
}


def rope_tables(length, size):
    half_size = size // 2
    frequency = ROPE_BASE ** (-np.arange(half_size) * (2.0 / size))
    angles = np.arange(length)[:, None] * frequency[None, :]
    return jnp.asarray(np.cos(angles), F32), jnp.asarray(np.sin(angles), F32)


def dot(a, b, da, db):
    return lax.dot_general(a, b, (((da,), (db,)), ((), ())), preferred_element_type=F32)


def attention_kernel(
    q_any, k_any, v_any, do_any, cos_any, sin_any, dq_any, kv_any, away_any, *scratch, block
):
    q_all, k_all, v_all, do_all, cos_ref, sin_ref, dq_all, kv_all, dk_acc, dv_acc = scratch[:10]
    in_sems, table_sems, out_sems = scratch[10:]
    length = q_all.shape[1]
    width = GROUP * HD
    inv_root = HD ** (-0.5)
    blocks = length // block
    first = lax.axis_index("c") == 0

    def loads(g):
        wide = pl.ds(pl.multiple_of(g * width, width), width)
        narrow = pl.ds(pl.multiple_of(g * HD, HD), HD)
        return [
            pltpu.make_async_copy(k_any.at[:, narrow], k_all.at[g], in_sems.at[g, 0]),
            pltpu.make_async_copy(q_any.at[:, wide], q_all.at[g], in_sems.at[g, 1]),
            pltpu.make_async_copy(v_any.at[:, narrow], v_all.at[g], in_sems.at[g, 2]),
            pltpu.make_async_copy(do_any.at[:, wide], do_all.at[g], in_sems.at[g, 3]),
        ]

    def stores(g):
        wide = pl.ds(pl.multiple_of(g * width, width), width)
        narrow = pl.ds(pl.multiple_of(g * HD, HD), HD)
        return [
            pltpu.make_async_copy(dq_all.at[g], dq_any.at[:, wide], out_sems.at[g, 0]),
            pltpu.make_async_copy(kv_all.at[g], kv_any.at[:, :, narrow], out_sems.at[g, 1]),
            pltpu.make_async_copy(kv_all.at[g, 1], away_any.at[:, narrow], out_sems.at[g, 2]),
        ]

    tables = [
        pltpu.make_async_copy(cos_any, cos_ref, table_sems.at[0]),
        pltpu.make_async_copy(sin_any, sin_ref, table_sems.at[1]),
    ]
    for load in loads(0) + loads(1) + tables + loads(2) + loads(3):
        load.start()
    rows = lax.broadcasted_iota(jnp.int32, (block, GROUP * block), 0)
    cols = lax.broadcasted_iota(jnp.int32, (block, GROUP * block), 1)
    keep = rows <= lax.rem(cols, block)

    def group(g, _):
        for load in loads(g):
            load.wait()
        k = k_all[g]
        v = v_all[g]
        for b in reversed(range(blocks)):
            end = (b + 1) * block
            part = slice(b * block, end)
            queries = jnp.concatenate(
                [q_all[g, part, j * HD : (j + 1) * HD] for j in range(GROUP)], axis=0
            )
            grads = jnp.concatenate(
                [do_all[g, part, j * HD : (j + 1) * HD] for j in range(GROUP)], axis=0
            )
            scores = dot(k[:end], queries, 1, 1)
            grad_prob = dot(v[:end], grads, 1, 1)
            diagonal = jnp.where(keep, scores[end - block :], -jnp.inf)
            if b:
                scores = jnp.concatenate([scores[: end - block], diagonal], axis=0)
            else:
                scores = diagonal
            top = jnp.max(scores, axis=0, keepdims=True)
            exponent = jnp.exp2((scores - top) * (LOG2E * inv_root))
            inv_sum = 1.0 / jnp.sum(exponent, axis=0, keepdims=True)
            delta = jnp.sum(exponent * grad_prob, axis=0, keepdims=True) * inv_sum
            prob_low = (exponent * inv_sum).astype(BF)
            grad_score = (exponent * (grad_prob - delta) * (inv_sum * inv_root)).astype(BF)
            dk = dot(grad_score, queries, 1, 0)
            dv = dot(prob_low, grads, 1, 0)
            if b == blocks - 1:
                dk_acc[...] = dk
                dv_acc[...] = dv
            else:
                dk_acc[:end, :] += dk
                dv_acc[:end, :] += dv
            dq = dot(grad_score, k[:end], 0, 0)
            for j in range(GROUP):
                dq_all[g, part, j * HD : (j + 1) * HD] = dq[j * block : (j + 1) * block].astype(BF)

        @pl.when(g == 0)
        def _():
            for load in tables:
                load.wait()

        key_grad = dk_acc[...]
        half = HD // 2
        cosine, sine = cos_ref[...], sin_ref[...]
        low, high = key_grad[:, :half], key_grad[:, half:]
        key_part = jnp.concatenate(
            [low * cosine + high * sine, high * cosine - low * sine], axis=1
        ).astype(BF)
        value_part = dv_acc[...].astype(BF)
        kv_all[g, 0] = jnp.where(first, key_part, value_part)
        kv_all[g, 1] = jnp.where(first, value_part, key_part)
        for store in stores(g):
            store.start()
        return 0

    lax.fori_loop(0, KVH, group, 0)
    for g in range(KVH):
        for store in stores(g):
            store.wait()


def attention(q, k, v, do, cosine, sine_tab):
    length = q.shape[0]
    width = GROUP * HD
    wide = pltpu.VMEM((KVH, length, width), BF)
    narrow = pltpu.VMEM((KVH, length, HD), BF)
    table = pltpu.VMEM((length, HD // 2), F32)
    total = pltpu.VMEM((length, HD), F32)
    return pl.pallas_call(
        functools.partial(attention_kernel, block=128),
        in_specs=[pl.BlockSpec(memory_space=pl.ANY)] * 6,
        out_specs=[pl.BlockSpec(memory_space=pl.ANY)] * 3,
        scratch_shapes=[
            wide,
            narrow,
            narrow,
            wide,
            table,
            table,
            wide,
            pltpu.VMEM((KVH, 2, length, HD), BF),
            total,
            total,
            pltpu.SemaphoreType.DMA((KVH, 4)),
            pltpu.SemaphoreType.DMA((2,)),
            pltpu.SemaphoreType.DMA((KVH, 3)),
        ],
        out_shape=[
            jax.ShapeDtypeStruct((length, KVH * width), BF),
            jax.ShapeDtypeStruct((2, length, KVH * HD), BF),
            jax.ShapeDtypeStruct((length, KVH * HD), BF),
        ],
        compiler_params=pltpu.CompilerParams(vmem_limit_bytes=ATTENTION_VMEM),
        name="attention",
    )(q, k, v, do, cosine, sine_tab)


def weight_kernel(
    own_ref, other_ref, kv_ref, kv_other_ref, *refs, scale, low
):
    outs, own, other, ka_ref, kb_ref, made, in_sems, kv_sems, out_sems = refs[:2], *refs[2:]
    zl, x, c, y, zh = (lax.axis_index(axis) for axis in AXES)
    cols = kb_ref.shape[1]
    width = own.shape[2]

    def source(e):
        along_x = (e // 2) * 4 + lax.bitwise_xor(x, low + 2 * (e % 2))
        along_z = lax.bitwise_xor(zl, low) * 4 + e
        start = jnp.where(c == 0, along_x, along_z) * width
        return pl.ds(pl.multiple_of(start, width), width)

    kv_load = pltpu.make_async_copy(kv_ref.at[0], ka_ref, kv_sems.at[0])
    kv_other_load = pltpu.make_async_copy(kv_other_ref, kb_ref, kv_sems.at[1])
    kv_load.start()
    loads = []
    for e in range(4):
        if e == 1:
            kv_other_load.start()
        for side, (ref, buffer) in enumerate(((own_ref, own), (other_ref, other))):
            load = pltpu.make_async_copy(ref.at[:, source(e)], buffer.at[e], in_sems.at[e, side])
            load.start()
            loads.append(load)
    for e in range(4):
        if e == 0:
            kv_load.wait()
        loads[2 * e].wait()
        value = dot(own[e], ka_ref[...], 0, 0)
        if e == 0:
            kv_other_load.wait()
        loads[2 * e + 1].wait()
        value += dot(other[e], kb_ref[...], 0, 0)
        value = (value * scale).astype(BF).reshape(2, 4, 2, 32, cols)
        to_zl = jnp.where(c == 0, e // 2, lax.bitwise_xor(zl, low))
        kx = jnp.where(c == 0, low + 2 * (e % 2), lax.bitwise_xor(e, x))
        for to_zh in range(2):
            kz = lax.bitwise_xor(to_zh, zh) * 2 + lax.bitwise_xor(to_zl, zl)
            first = jnp.where(c == 0, kx, kz) >> 1
            second = jnp.where(c == 0, kz, kx)
            for to_c in range(2):
                for to_y in range(4):
                    kc, ky = lax.bitwise_xor(to_c, c), lax.bitwise_xor(to_y, y)
                    made[first, second, ky, kc] = value[to_c, to_y, to_zh]
            for k in range(2):

                @pl.when(first == k)
                def _():
                    pltpu.make_async_copy(
                        made.at[k, second], outs[k].at[second], out_sems.at[k, second]
                    ).start()

    for k in range(2):
        for second in range(4):
            pltpu.make_async_copy(
                made.at[k, second], outs[k].at[second], out_sems.at[k, second]
            ).wait()


def weight_terms(own, other, kv, kv_other, scale, low):
    tokens, width = own.shape
    cols = kv.shape[2]
    shape = (4, 4, 2, 32, cols)
    anywhere = pl.BlockSpec(memory_space=pl.ANY)
    return pl.pallas_call(
        functools.partial(weight_kernel, scale=scale, low=low),
        in_specs=[anywhere] * 4,
        out_specs=[anywhere] * 2,
        scratch_shapes=[
            pltpu.VMEM((4, tokens, width // 8), BF),
            pltpu.VMEM((4, tokens, width // 8), BF),
            pltpu.VMEM((tokens, cols), BF),
            pltpu.VMEM((tokens, cols), BF),
            pltpu.VMEM((2,) + shape, BF),
            pltpu.SemaphoreType.DMA((4, 2)),
            pltpu.SemaphoreType.DMA((2,)),
            pltpu.SemaphoreType.DMA((2, 4)),
        ],
        out_shape=[jax.ShapeDtypeStruct(shape, BF) for _ in range(2)],
        compiler_params=pltpu.CompilerParams(vmem_limit_bytes=WEIGHT_VMEM),
        name="weight_terms",
    )(own, other, kv, kv_other)


def input_kernel(place, *refs):
    kvs, blocks, out_ref = refs[:8], refs[8:16], refs[-1]
    kv = jnp.concatenate([r[0] for r in kvs], axis=1)
    weights = jnp.concatenate([r[...] for r in blocks], axis=1)
    out_ref[...] = dot(kv, weights, 1, 1).astype(BF)


def input_grads(place, kv, own_proj, blocks, turn, earlier=None):
    length = kv.shape[1]
    depth = own_proj.shape[0]
    tile = INPUT_TILE
    half = depth // tile // 2

    def kv_map(j):
        k, h = j % 4, j // 4

        def index(i, p):
            node = lax.bitwise_xor(p[1], k) * 2 + lax.bitwise_xor(p[2], h)
            return (lax.bitwise_xor(node // 4, p[0]), 0, node & 3)

        return index

    def own_map(i, p):
        return (lax.bitwise_xor(p[0], turn) * half + i, 0)

    def out_map(i, p):
        return (0, lax.bitwise_xor(p[0], turn) * half + i)

    in_specs = [pl.BlockSpec((1, length, HD), kv_map(j)) for j in range(8)]
    in_specs += [pl.BlockSpec((tile, HD), own_map)]
    in_specs += [pl.BlockSpec((tile, HD), lambda i, p: (i, 0)) for _ in range(7)]
    operands = [place, *([kv] * 8), own_proj, *blocks]
    aliases = {}
    if earlier is not None:
        in_specs += [pl.BlockSpec(memory_space=pl.ANY)]
        aliases = {len(operands): 0}
        operands += [earlier]
    return pl.pallas_call(
        input_kernel,
        grid_spec=pltpu.PrefetchScalarGridSpec(
            num_scalar_prefetch=1,
            grid=(half,),
            in_specs=in_specs,
            out_specs=pl.BlockSpec((length, tile), out_map),
        ),
        out_shape=jax.ShapeDtypeStruct((length, depth), BF),
        input_output_aliases=aliases,
        compiler_params=pltpu.CompilerParams(vmem_limit_bytes=INPUT_VMEM),
        name="input_grads",
    )(*operands)


def send(value, pairs):
    return lax.ppermute(value, AXES, pairs)


def exchange(arrays, pairs):
    parts = [sum(a[k].astype(F32) for a in arrays) for k in range(4)]
    return [parts[0]] + [send(parts[k].astype(BF), pairs[k]) for k in (1, 2, 3)]


def local(normed, queries, keys, values, attn_grad, kv_proj):
    length, width = normed.shape
    c = lax.axis_index("c")
    place = jnp.stack([c, lax.axis_index("y"), lax.axis_index("zh")]).astype(jnp.int32)
    tokens = length * lax.axis_size(AXES)
    cosine, sine_tab = rope_tables(length, HD)

    half = jnp.where(c == 0, kv_proj[: width // 2], kv_proj[width // 2 :])
    normed_other = send(normed, PARTNER)
    near = [send(half, ALONG_Y[k]) for k in (1, 2, 3)]
    query_grad, kv, away = attention(queries, keys, values, attn_grad, cosine, sine_tab)
    kv_other = send(away, PARTNER)
    across = send(half, Z_HALF)
    scale = tokens ** (-0.5)
    odd = weight_terms(normed, normed_other, kv, kv_other, scale, 1)
    first1 = send(odd[0], FIRST[1])
    first3 = send(odd[1], FIRST[3])
    even = weight_terms(normed, normed_other, kv, kv_other, scale, 0)
    first2 = send(even[1], FIRST[2])
    got = [even[0], first1, first2, first3]

    far = [send(across, ALONG_Y[k]) for k in (1, 2, 3)]
    mine = near + [across] + far
    theirs = [send(block, PARTNER) for block in mine[:4]]
    theirs += [send(block, PARTNER) for block in mine[4:]]
    input_grad = input_grads(place, kv, kv_proj, mine, 0)
    input_grad = input_grads(place, kv, kv_proj, theirs, 1, input_grad)

    got = exchange(got, SECOND)
    got = exchange(got, ALONG_Y)
    total = sum(g.astype(F32) for g in got)
    part, other = total[0], send(total[1], PARTNER)
    weight_grad = jnp.where(
        c == 0, jnp.concatenate([part, other], axis=1), jnp.concatenate([other, part], axis=1)
    )
    return (query_grad, input_grad, weight_grad)


def solution(mesh):
    mesh = Mesh(mesh.devices.reshape(2, 4, 2, 4, 2), AXES)
    spec = P(AXES, None)
    return jax.shard_map(
        local,
        mesh=mesh,
        in_specs=(spec, spec, spec, spec, spec, P(None, ("y", "zh"))),
        out_specs=(spec, spec, spec),
        check_vma=False,
    )
```

```python
import functools

import jax
import jax.numpy as jnp
import numpy as np
from jax import lax
from jax.experimental import pallas as pl
from jax.experimental.pallas import tpu as pltpu
from jax.sharding import Mesh
from jax.sharding import PartitionSpec as P


KVH = 4
HD = 128
GROUP = 4
ROPE_BASE = 500000.0
LOG2E = 1.4426950408889634
INPUT_TILE = 1024
ATTENTION_VMEM = 60 << 20
WEIGHT_VMEM = 58 << 20
INPUT_VMEM = 24 << 20
AXES = ("zl", "x", "c", "y", "zh")
F32 = jnp.float32
BF = jnp.bfloat16


def permutation(move):
    pairs = []
    for zl in range(2):
        for x in range(4):
            for c in range(2):
                for y in range(4):
                    for zh in range(2):
                        source = ((zl * 4 + x) * 2 + c) * 8 + y * 2 + zh
                        tx, tc, ty, tz = move(x, c, y, zh * 2 + zl)
                        pairs.append((source, (((tz % 2) * 4 + tx) * 2 + tc) * 8 + ty * 2 + tz // 2))
    return pairs


PARTNER = permutation(lambda x, c, y, z: (x, 1 - c, y, z))
BESIDE = permutation(lambda x, c, y, z: (x, c, y ^ (3 if c else 1), z))
Z_HALF = permutation(lambda x, c, y, z: (x, c, y, z ^ 2))
ALONG_Y = {k: permutation(lambda x, c, y, z: (x, c, y ^ k, z)) for k in (1, 2, 3)}
FIRST = {
    k: permutation(lambda x, c, y, z: (x ^ k, c, y, z) if c == 0 else (x, c, y, z ^ k))
    for k in (1, 2, 3)
}
SECOND = {
    k: permutation(lambda x, c, y, z: (x, c, y, z ^ k) if c == 0 else (x ^ k, c, y, z))
    for k in (1, 2, 3)
}


def rope_tables(length, size):
    half_size = size // 2
    frequency = ROPE_BASE ** (-np.arange(half_size) * (2.0 / size))
    angles = np.arange(length)[:, None] * frequency[None, :]
    return jnp.asarray(np.cos(angles), F32), jnp.asarray(np.sin(angles), F32)


def dot(a, b, da, db):
    return lax.dot_general(a, b, (((da,), (db,)), ((), ())), preferred_element_type=F32)


def attention_kernel(
    q_ref, k_ref, v_ref, do_ref, cos_ref, sin_ref, dq_ref, kv_ref, away_ref, dk_acc, dv_acc, *, block
):
    length = q_ref.shape[0]
    inv_root = HD ** (-0.5)
    blocks = length // block
    k = k_ref[...]
    v = v_ref[...]
    rows = lax.broadcasted_iota(jnp.int32, (block, GROUP * block), 0)
    cols = lax.broadcasted_iota(jnp.int32, (block, GROUP * block), 1)
    keep = rows <= lax.rem(cols, block)
    for b in reversed(range(blocks)):
        end = (b + 1) * block
        part = slice(b * block, end)
        queries = jnp.concatenate([q_ref[part, j * HD : (j + 1) * HD] for j in range(GROUP)], axis=0)
        grads = jnp.concatenate([do_ref[part, j * HD : (j + 1) * HD] for j in range(GROUP)], axis=0)
        scores = dot(k[:end], queries, 1, 1)
        grad_prob = dot(v[:end], grads, 1, 1)
        diagonal = jnp.where(keep, scores[end - block :], -jnp.inf)
        if b:
            scores = jnp.concatenate([scores[: end - block], diagonal], axis=0)
        else:
            scores = diagonal
        top = jnp.max(scores, axis=0, keepdims=True)
        exponent = jnp.exp2((scores - top) * (LOG2E * inv_root))
        inv_sum = 1.0 / jnp.sum(exponent, axis=0, keepdims=True)
        delta = jnp.sum(exponent * grad_prob, axis=0, keepdims=True) * inv_sum
        prob_low = (exponent * inv_sum).astype(BF)
        grad_score = (exponent * (grad_prob - delta) * (inv_sum * inv_root)).astype(BF)
        dk = dot(grad_score, queries, 1, 0)
        dv = dot(prob_low, grads, 1, 0)
        if b == blocks - 1:
            dk_acc[...] = dk
            dv_acc[...] = dv
        else:
            dk_acc[:end, :] += dk
            dv_acc[:end, :] += dv
        dq = dot(grad_score, k[:end], 0, 0)
        for j in range(GROUP):
            dq_ref[part, j * HD : (j + 1) * HD] = dq[j * block : (j + 1) * block].astype(BF)
    key_grad = dk_acc[...]
    half = HD // 2
    cosine, sine = cos_ref[...], sin_ref[...]
    low, high = key_grad[:, :half], key_grad[:, half:]
    key_part = jnp.concatenate([low * cosine + high * sine, high * cosine - low * sine], axis=1).astype(BF)
    value_part = dv_acc[...].astype(BF)
    first = lax.axis_index("c") == 0
    stay = jnp.where(first, key_part, value_part)
    away = jnp.where(first, value_part, key_part)
    kv_ref[0] = stay
    kv_ref[1] = away
    away_ref[...] = away


def attention(q, k, v, do, cosine, sine_tab):
    length = q.shape[0]
    width = GROUP * HD
    return pl.pallas_call(
        functools.partial(attention_kernel, block=128),
        grid=(KVH,),
        in_specs=[
            pl.BlockSpec((length, width), lambda g: (0, g)),
            pl.BlockSpec((length, HD), lambda g: (0, g)),
            pl.BlockSpec((length, HD), lambda g: (0, g)),
            pl.BlockSpec((length, width), lambda g: (0, g)),
            pl.BlockSpec((length, HD // 2), lambda g: (0, 0)),
            pl.BlockSpec((length, HD // 2), lambda g: (0, 0)),
        ],
        out_specs=[
            pl.BlockSpec((length, width), lambda g: (0, g)),
            pl.BlockSpec((2, length, HD), lambda g: (0, 0, g)),
            pl.BlockSpec((length, HD), lambda g: (0, g)),
        ],
        scratch_shapes=[pltpu.VMEM((length, HD), F32), pltpu.VMEM((length, HD), F32)],
        out_shape=[
            jax.ShapeDtypeStruct((length, KVH * width), BF),
            jax.ShapeDtypeStruct((2, length, KVH * HD), BF),
            jax.ShapeDtypeStruct((length, KVH * HD), BF),
        ],
        compiler_params=pltpu.CompilerParams(vmem_limit_bytes=ATTENTION_VMEM),
        name="attention",
    )(q, k, v, do, cosine, sine_tab)


def weight_kernel(
    own_ref, other_ref, kv_ref, kv_other_ref, *refs, scale, low
):
    outs, own, other, ka_ref, kb_ref, made, in_sems, kv_sems, out_sems = refs[:2], *refs[2:]
    zl, x, c, y, zh = (lax.axis_index(axis) for axis in AXES)
    cols = kb_ref.shape[1]
    width = own.shape[2]

    def source(e):
        along_x = (e // 2) * 4 + lax.bitwise_xor(x, low + 2 * (e % 2))
        along_z = lax.bitwise_xor(zl, low) * 4 + e
        start = jnp.where(c == 0, along_x, along_z) * width
        return pl.ds(pl.multiple_of(start, width), width)

    kv_load = pltpu.make_async_copy(kv_ref.at[0], ka_ref, kv_sems.at[0])
    kv_other_load = pltpu.make_async_copy(kv_other_ref, kb_ref, kv_sems.at[1])
    loads = []
    for e in range(4):
        for side, (ref, buffer) in enumerate(((own_ref, own), (other_ref, other))):
            load = pltpu.make_async_copy(ref.at[:, source(e)], buffer.at[e], in_sems.at[e, side])
            loads.append(load)
    for load in (kv_load, loads[0], kv_other_load, *loads[1:4]):
        load.start()
    for e in range(4):
        if e == 0:
            kv_load.wait()
        loads[2 * e].wait()
        value = dot(own[e], ka_ref[...], 0, 0)
        if e == 0:
            kv_other_load.wait()
        loads[2 * e + 1].wait()
        if e < 2:
            loads[2 * e + 4].start()
            loads[2 * e + 5].start()
        value += dot(other[e], kb_ref[...], 0, 0)
        value = (value * scale).astype(BF).reshape(2, 4, 2, 32, cols)
        to_zl = jnp.where(c == 0, e // 2, lax.bitwise_xor(zl, low))
        kx = jnp.where(c == 0, low + 2 * (e % 2), lax.bitwise_xor(e, x))
        for to_zh in range(2):
            kz = lax.bitwise_xor(to_zh, zh) * 2 + lax.bitwise_xor(to_zl, zl)
            first = jnp.where(c == 0, kx, kz) >> 1
            second = jnp.where(c == 0, kz, kx)
            for to_c in range(2):
                for to_y in range(4):
                    kc, ky = lax.bitwise_xor(to_c, c), lax.bitwise_xor(to_y, y)
                    made[first, second, ky, kc] = value[to_c, to_y, to_zh]
            for k in range(2):

                @pl.when(first == k)
                def _():
                    pltpu.make_async_copy(
                        made.at[k, second], outs[k].at[second], out_sems.at[k, second]
                    ).start()

    for k in range(2):
        for second in range(4):
            pltpu.make_async_copy(
                made.at[k, second], outs[k].at[second], out_sems.at[k, second]
            ).wait()


def weight_terms(own, other, kv, kv_other, scale, low):
    tokens, width = own.shape
    cols = kv.shape[2]
    shape = (4, 4, 2, 32, cols)
    anywhere = pl.BlockSpec(memory_space=pl.ANY)
    return pl.pallas_call(
        functools.partial(weight_kernel, scale=scale, low=low),
        in_specs=[anywhere] * 4,
        out_specs=[anywhere] * 2,
        scratch_shapes=[
            pltpu.VMEM((4, tokens, width // 8), BF),
            pltpu.VMEM((4, tokens, width // 8), BF),
            pltpu.VMEM((tokens, cols), BF),
            pltpu.VMEM((tokens, cols), BF),
            pltpu.VMEM((2,) + shape, BF),
            pltpu.SemaphoreType.DMA((4, 2)),
            pltpu.SemaphoreType.DMA((2,)),
            pltpu.SemaphoreType.DMA((2, 4)),
        ],
        out_shape=[jax.ShapeDtypeStruct(shape, BF) for _ in range(2)],
        compiler_params=pltpu.CompilerParams(vmem_limit_bytes=WEIGHT_VMEM),
        name="weight_terms",
    )(own, other, kv, kv_other)


def input_kernel(place, *refs):
    kvs, blocks, out_ref = refs[:8], refs[8:16], refs[-1]
    kv = jnp.concatenate([r[0] for r in kvs], axis=1)
    weights = jnp.concatenate([r[...] for r in blocks], axis=1)
    out_ref[...] = dot(kv, weights, 1, 1).astype(BF)


def input_grads(place, kv, whole, parts, turn, earlier=None):
    length = kv.shape[1]
    depth = whole[0].shape[0]
    tile = INPUT_TILE
    half = depth // tile // 2
    steps = (0, 1, 3, 2, 0, 1, 2, 3)

    def kv_map(j):
        def index(i, p):
            step = jnp.where(p[0] == 0, steps[j], 4 - steps[j]) if j in (1, 2) else steps[j]
            node = lax.bitwise_xor(p[1], step) * 2 + lax.bitwise_xor(p[2], int(j > 3))
            return (lax.bitwise_xor(node // 4, p[0]), 0, node & 3)

        return index

    def whole_map(i, p):
        return (lax.bitwise_xor(p[0], turn) * half + i, 0)

    def out_map(i, p):
        return (0, lax.bitwise_xor(p[0], turn) * half + i)

    in_specs = [pl.BlockSpec((1, length, HD), kv_map(j)) for j in range(8)]
    in_specs += [pl.BlockSpec((tile, HD), whole_map) for _ in whole]
    in_specs += [pl.BlockSpec((tile, HD), lambda i, p: (i, 0)) for _ in parts]
    operands = [place, *([kv] * 8), *whole, *parts]
    aliases = {}
    if earlier is not None:
        in_specs += [pl.BlockSpec(memory_space=pl.ANY)]
        aliases = {len(operands): 0}
        operands += [earlier]
    return pl.pallas_call(
        input_kernel,
        grid_spec=pltpu.PrefetchScalarGridSpec(
            num_scalar_prefetch=1,
            grid=(half,),
            in_specs=in_specs,
            out_specs=pl.BlockSpec((length, tile), out_map),
        ),
        out_shape=jax.ShapeDtypeStruct((length, depth), BF),
        input_output_aliases=aliases,
        compiler_params=pltpu.CompilerParams(vmem_limit_bytes=INPUT_VMEM),
        name="input_grads",
    )(*operands)


def send(value, pairs):
    return lax.ppermute(value, AXES, pairs)


def exchange(arrays, pairs):
    parts = [sum(a[k].astype(F32) for a in arrays) for k in range(4)]
    return [parts[0]] + [send(parts[k].astype(BF), pairs[k]) for k in (1, 2, 3)]


def local(normed, queries, keys, values, attn_grad, kv_proj):
    length, width = normed.shape
    c = lax.axis_index("c")
    place = jnp.stack([c, lax.axis_index("y"), lax.axis_index("zh")]).astype(jnp.int32)
    tokens = length * lax.axis_size(AXES)
    cosine, sine_tab = rope_tables(length, HD)

    beside = send(kv_proj, BESIDE)
    normed_other = send(normed, PARTNER)
    query_grad, kv, away = attention(queries, keys, values, attn_grad, cosine, sine_tab)
    kv_other = send(away, PARTNER)
    late_proj = lax.optimization_barrier((kv_proj, away))[0]
    half = jnp.where(c == 0, late_proj[: width // 2], late_proj[width // 2 :])
    across = send(half, Z_HALF)
    near2 = send(half, ALONG_Y[2])
    scale = tokens ** (-0.5)
    odd = weight_terms(normed, normed_other, kv, kv_other, scale, 1)
    first1 = send(odd[0], FIRST[1])
    first3 = send(odd[1], FIRST[3])
    even = weight_terms(normed, normed_other, kv, kv_other, scale, 0)
    first2 = send(even[1], FIRST[2])
    early = lax.optimization_barrier(sum(g.astype(F32) for g in (even[0], first1, first3)))
    got = [early, first2]

    far = [send(across, ALONG_Y[k]) for k in (1, 2, 3)]
    whole = [kv_proj, beside, send(beside, PARTNER)]
    mine = [near2, across] + far
    theirs = [send(block, PARTNER) for block in mine[:2]]
    theirs += [send(block, PARTNER) for block in mine[2:]]
    input_grad = input_grads(place, kv, whole, mine, 0)
    input_grad = input_grads(place, kv, whole, theirs, 1, input_grad)

    got = exchange(got, SECOND)
    got = exchange(got, ALONG_Y)
    other = send(sum(g[1].astype(F32) for g in got), PARTNER)
    part = sum(g[0].astype(F32) for g in got)
    weight_grad = jnp.where(
        c == 0, jnp.concatenate([part, other], axis=1), jnp.concatenate([other, part], axis=1)
    )
    return (query_grad, input_grad, weight_grad)


def solution(mesh):
    mesh = Mesh(mesh.devices.reshape(2, 4, 2, 4, 2), AXES)
    spec = P(AXES, None)
    return jax.shard_map(
        local,
        mesh=mesh,
        in_specs=(spec, spec, spec, spec, spec, P(None, ("y", "zh"))),
        out_specs=(spec, spec, spec),
        check_vma=False,
    )
```
